32 devices in a mesh: gx: 4 (over y, x), gy: 2 (over core), gz: 4 (over z).
Axes of the slice: x: 2, y: 2, z: 4, core: 2. Of those that a mesh axis runs over, the one named last changes fastest.
Arguments:
- correction: float32 [64, 64, 512], P('gz', 'gx', 'gy'), may hold values from -6 to 6
- residual: float32 [64, 64, 512], P('gz', 'gx', 'gy'), may hold values from -4 to 6
- state: float32 [64, 64, 512], P('gz', 'gx', 'gy'), may hold values from -1 to 1
- spacing_level: int32 [64], replicated, may hold values from 0 to 3
- line_colour: int32 [64, 512], P('gx', 'gy'), may hold values from 0 to 1
Outputs:
- smoothed: float32 [64, 64, 512], P('gz', 'gx', 'gy')
The draws below stay inside these ranges and needn't reach their ends.
All inputs are finite; a program needn't handle non-finite values.
Results may differ from the reference program's by a relative error of at most 0.0003.
Values sent between devices are 32-bit elements; how exact they have to be, the bound alone decides.
A program may use at most 64 MiB of HBM per device.

```python
import jax
import jax.numpy as jnp
from jax import lax

NZ = 64
NX = 64
NY = 512


def draw_residual(key, part):
    key_noise = jax.random.fold_in(key, 1)
    noise_part = jax.random.normal(key_noise, (NZ, NX, NY), jnp.float32)
    return jnp.clip(1.0 + noise_part, -4.0, 6.0)


def with_ends(drawn, rng, least, largest):
    longest = drawn.shape.index(max(drawn.shape))
    spots = []
    for shift in (0, 1):
        where = [jax.random.randint(jax.random.fold_in(rng, axis), (), 0, length) for axis, length in enumerate(drawn.shape)]
        where[longest] = (where[longest] + shift) % drawn.shape[longest]
        spots.append(tuple(where))
    return drawn.at[spots[0]].set(least).at[spots[1]].set(largest)


def steps_of(stream_key, extent, shards, low, top_value):
    loudness = 1.0
    for dim, blocks in shards:
        steps = jax.random.uniform(jax.random.fold_in(jax.random.fold_in(stream_key, 6), dim), (blocks,), jnp.float32, low / len(shards), top_value / len(shards))
        loudness = loudness * jnp.repeat(jnp.exp(steps), extent[dim] // blocks).reshape((-1,) + (1,) * (len(extent) - 1 - dim))
    return loudness


def noise(rng, shape, spread, most, cuts=(), kind=jnp.bfloat16):
    result = jax.random.normal(rng, shape, jnp.float32) * spread
    if len(cuts) > 0:
        result = steps_of(rng, shape, cuts, -0.22, 0.18) * result
    return jnp.clip(result, min=-most, max=most).astype(kind)


def setup_inputs(seed: int = 0) -> dict:
    arg_keys = jax.random.split(jax.random.key(seed), 6)
    return {
        "correction": noise(arg_keys[0], (NZ, NX, NY), 1.0, 6.0, ((0, 4), (1, 4), (2, 2)), jnp.float32),
        "residual": draw_residual(jax.random.fold_in(arg_keys[5], 71), 0),
        "state": jnp.clip(jax.random.uniform(arg_keys[2], (NZ, NX, NY), jnp.float32, -1.0, 1.0) * steps_of(arg_keys[2], (NZ, NX, NY), ((0, 4), (1, 4), (2, 2)), -0.4, 0.0), -1.0, 1.0),
        "spacing_level": with_ends(jax.random.randint(arg_keys[3], (NZ,), 0, 4), jax.random.fold_in(arg_keys[3], 1), 0, 3).astype(jnp.int32),
        "line_colour": with_ends(jax.random.randint(arg_keys[4], (NX, NY), 0, 2), jax.random.fold_in(arg_keys[4], 1), 0, 1).astype(jnp.int32),
    }


coef_z = 1000.0
coef_x = 0.3
coef_y = 0.2
bratu_lambda = 0.2


def face_coupling(spacing_level):
    spacing_cells = 0.8 * jnp.power(1.3, spacing_level.astype(jnp.float32))
    inner_faces = coef_z * 2.0 / (spacing_cells[:-1] + spacing_cells[1:])
    nothing = jnp.zeros((1,), jnp.float32)
    face_low = jnp.concatenate([nothing, inner_faces])
    face_high = jnp.concatenate([inner_faces, nothing])
    return spacing_cells, face_low, face_high


def thomas_solve(below_coef, centre, above_coef, source):
    def forward(state_carry, row_data):
        prev_ratio, prev_value = state_carry
        low_term, mid_term, high_term, src_term = row_data
        pivot_value = mid_term - low_term * prev_ratio
        ratio_now = high_term / pivot_value
        value_now = (src_term - low_term * prev_value) / pivot_value
        return (ratio_now, value_now), (ratio_now, value_now)

    blank = jnp.zeros(centre.shape[1:], jnp.float32)
    unused_end, (ratios, values) = lax.scan(forward, (blank, blank), (below_coef, centre, above_coef, source))

    def backward(next_value, row_data):
        ratio_now, value_now = row_data
        result_now = value_now - ratio_now * next_value
        return result_now, result_now

    unused_start, solution = lax.scan(backward, blank, (ratios, values), reverse=True)
    return solution


def reference(correction, residual, state, spacing_level, line_colour):
    spacing_cells, face_low, face_high = face_coupling(spacing_level)
    column = spacing_cells[:, None, None]
    centre = (face_low + face_high)[:, None, None] + column * (2.0 * coef_x + 2.0 * coef_y - bratu_lambda * jnp.exp(state))
    iterate = correction
    for colour in range(2):
        padded = jnp.pad(iterate, ((0, 0), (1, 1), (1, 1)))
        beside = coef_x * (padded[:, 2:, 1:-1] + padded[:, :-2, 1:-1]) + coef_y * (padded[:, 1:-1, 2:] + padded[:, 1:-1, :-2])
        source = column * (residual + beside)
        solved = thomas_solve(-face_low, centre, -face_high, source)
        iterate = jnp.where((line_colour == colour)[None], solved, iterate)
    return iterate
```

```python
import functools

import jax
import jax.numpy as jnp
import numpy as np
from jax import lax
from jax.experimental import pallas as pl
from jax.experimental.pallas import tpu as pltpu
from jax.sharding import PartitionSpec as P

coef_z = 1000.0
coef_x = 0.3
coef_y = 0.2
bratu_lambda = 0.2
LANES = 128
MESH = pl.DeviceIdType.MESH


def relax_kernel(
    counts,
    level_ref,
    corr_hbm,
    res_hbm,
    state_hbm,
    colour_hbm,
    out_ref,
    corr,
    res,
    state,
    colour,
    iterate,
    inv,
    low_w,
    high_w,
    src,
    local,
    x_send,
    x_recv,
    y_recv,
    up_send,
    up_recv,
    down_send,
    down_recv,
    load_sem,
    x_send_sem,
    x_recv_sem,
    y_send_sem,
    y_recv_sem,
    up_send_sem,
    up_recv_sem,
    down_send_sem,
    down_recv_sem,
):
    nx, ny, nz = counts
    depth, wide_x, wide_y = corr.shape
    px, py, pz = (lax.axis_index(a) for a in ("gx", "gy", "gz"))
    total = depth * nz

    axes = (("gx", px, nx), ("gy", py, ny), ("gz", pz, nz))
    barrier = pltpu.get_barrier_semaphore()
    present = jnp.int32(0)
    for axis, place, count in axes:
        present = present + jnp.where(place > 0, 1, 0) + jnp.where(place < count - 1, 1, 0)

        @pl.when(place > 0)
        def _():
            pl.semaphore_signal(barrier, inc=1, device_id={axis: place - 1}, device_id_type=MESH)

        @pl.when(place < count - 1)
        def _():
            pl.semaphore_signal(barrier, inc=1, device_id={axis: place + 1}, device_id_type=MESH)

    loads = [
        pltpu.make_async_copy(a, b, load_sem.at[n])
        for n, (a, b) in enumerate(
            ((state_hbm, state), (corr_hbm, corr), (res_hbm, res), (colour_hbm, colour))
        )
    ]
    for load in loads:
        load.start()

    for side, gone in ((0, px == 0), (1, px == nx - 1)):

        @pl.when(gone)
        def _():
            for turn in range(2):
                x_recv[turn, side] = jnp.zeros((depth, wide_y), jnp.float32)

    for side, gone in ((0, py == 0), (1, py == ny - 1)):

        @pl.when(gone)
        def _():
            for turn in range(2):
                y_recv[turn, side] = jnp.zeros((depth, wide_x, LANES), jnp.float32)

    @pl.when(pz == 0)
    def _():
        up_recv[...] = jnp.zeros(up_recv.shape, jnp.float32)

    @pl.when(pz == nz - 1)
    def _():
        down_recv[...] = jnp.zeros(down_recv.shape, jnp.float32)

    def spread(tile):
        row = jnp.concatenate([tile] * (wide_y // LANES), 1)
        return jnp.concatenate([row] * (wide_x // 8), 0)

    powers = [np.float32(0.8) * np.float32(1.3**n) for n in range(4)]

    def spacing_at(index):
        level = level_ref[index]
        value = jnp.where(level == 0, powers[0], powers[1])
        value = jnp.where(level == 2, powers[2], value)
        return jnp.where(level == 3, powers[3], value)

    base = pz * depth
    spacing = [spacing_at(base + i) for i in range(depth)]
    before = spacing_at(jnp.maximum(base - 1, 0))
    after = spacing_at(jnp.minimum(base + depth, total - 1))
    chain = [before] + spacing + [after]
    faces = []
    for i in range(depth + 1):
        face = coef_z * 2.0 / jnp.full((8, LANES), chain[i] + chain[i + 1], jnp.float32)
        if i == 0:
            face = jnp.where(pz == 0, 0.0, face)
        if i == depth:
            face = jnp.where(pz == nz - 1, 0.0, face)
        faces.append(spread(face))
    face_first, face_last = faces[0], faces[depth]

    loads[0].wait()
    for i in range(depth):
        state[i] = (faces[i] + faces[i + 1]) + spacing[i] * (
            2.0 * coef_x + 2.0 * coef_y - bratu_lambda * jnp.exp(state[i])
        )
    forward = 1.0 / state[0]
    backward = 1.0 / state[depth - 1]
    inv[0] = forward
    low_w[depth - 1] = backward
    for i in range(1, depth):
        forward = 1.0 / (state[i] - faces[i] * faces[i] * forward)
        inv[i] = forward
        j = depth - 1 - i
        backward = 1.0 / (state[j] - faces[j + 1] * faces[j + 1] * backward)
        low_w[j] = backward
    high_w[depth - 1] = forward
    for i in range(1, depth):
        backward = backward * faces[i] * low_w[i]
        low_w[i] = backward
        j = depth - 1 - i
        forward = forward * faces[j + 1] * inv[j]
        high_w[j] = forward

    def x_copy(turn, side):
        return pltpu.make_async_remote_copy(
            src_ref=x_send.at[turn, side],
            dst_ref=x_recv.at[turn, 1 - side],
            send_sem=x_send_sem.at[turn, side],
            recv_sem=x_recv_sem.at[turn, 1 - side],
            device_id={"gx": px - 1 if side == 0 else px + 1},
            device_id_type=MESH,
        )

    def y_copy(turn, side):
        whole = corr if turn == 0 else iterate
        start = 0 if side == 0 else wide_y - LANES
        return pltpu.make_async_remote_copy(
            src_ref=whole.at[:, :, pl.ds(start, LANES)],
            dst_ref=y_recv.at[turn, 1 - side],
            send_sem=y_send_sem.at[turn, side],
            recv_sem=y_recv_sem.at[turn, 1 - side],
            device_id={"gy": py - 1 if side == 0 else py + 1},
            device_id_type=MESH,
        )

    def up_copy(slot):
        return pltpu.make_async_remote_copy(
            src_ref=up_send.at[slot],
            dst_ref=up_recv.at[slot],
            send_sem=up_send_sem.at[slot],
            recv_sem=up_recv_sem.at[slot],
            device_id={"gz": pz + 1},
            device_id_type=MESH,
        )

    def down_copy(slot):
        return pltpu.make_async_remote_copy(
            src_ref=down_send.at[slot],
            dst_ref=down_recv.at[slot],
            send_sem=down_send_sem.at[slot],
            recv_sem=down_recv_sem.at[slot],
            device_id={"gz": pz - 1},
            device_id_type=MESH,
        )

    def on_sides(place, count, action):
        for side, there in ((0, place > 0), (1, place < count - 1)):

            @pl.when(there)
            def _():
                action(side)

    def send_halos(turn):
        on_sides(px, nx, lambda side: x_copy(turn, side).start())
        on_sides(py, ny, lambda side: y_copy(turn, side).start())

    def wait_halos(turn):
        on_sides(py, ny, lambda side: y_copy(turn, 1 - side).wait_recv())
        on_sides(px, nx, lambda side: x_copy(turn, 1 - side).wait_recv())

    loads[1].wait()
    for i in range(depth):
        x_send[0, 0, pl.ds(i, 1)] = corr[i, pl.ds(0, 1)]
        x_send[0, 1, pl.ds(i, 1)] = corr[i, pl.ds(wide_x - 1, 1)]
    pl.semaphore_wait(barrier, present)
    send_halos(0)

    first_both = low_w[depth - 1]

    def up_factor():
        ratio = up_recv[0]
        gain = first_both * face_first / (1.0 - low_w[0] * face_first * ratio)
        return ratio, gain, face_last * (high_w[depth - 1] + first_both * gain * ratio)

    def down_factor():
        ratio = down_recv[0]
        gain = first_both * face_last / (1.0 - high_w[depth - 1] * face_last * ratio)
        return ratio, gain, face_first * (low_w[0] + first_both * gain * ratio)

    @pl.when((pz == 0) & (pz < nz - 1))
    def _():
        up_send[0] = up_factor()[2]
        up_copy(0).start()

    @pl.when((pz == nz - 1) & (pz > 0))
    def _():
        down_send[0] = down_factor()[2]
        down_copy(0).start()

    loads[2].wait()
    loads[3].wait()

    rows = lax.broadcasted_iota(jnp.int32, (wide_x, wide_y), 0)
    columns = lax.broadcasted_iota(jnp.int32, (wide_x, wide_y), 1)
    narrow = lax.broadcasted_iota(jnp.int32, (wide_x, LANES), 1)
    x_first, x_last = rows == 0, rows == wide_x - 1
    y_first, y_last = columns == 0, columns == wide_y - 1

    for turn in range(2):
        held = corr if turn == 0 else iterate
        for i in range(depth):
            plane = held[i]
            beside = coef_x * (
                jnp.where(x_first, 0.0, pltpu.roll(plane, 1, 0))
                + jnp.where(x_last, 0.0, pltpu.roll(plane, wide_x - 1, 0))
            ) + coef_y * (
                jnp.where(y_first, 0.0, pltpu.roll(plane, 1, 1))
                + jnp.where(y_last, 0.0, pltpu.roll(plane, wide_y - 1, 1))
            )
            src[i] = spacing[i] * (res[i] + beside)
        wait_halos(turn)
        first_value = jnp.zeros((wide_x, wide_y), jnp.float32)
        last_value = first_value
        for i in range(depth):
            halo_x = jnp.where(
                x_first,
                x_recv[turn, 0, pl.ds(i, 1)],
                jnp.where(x_last, x_recv[turn, 1, pl.ds(i, 1)], 0.0),
            )
            halo_low = jnp.where(narrow == 0, pltpu.roll(y_recv[turn, 0, i], 1, 1), 0.0)
            halo_high = jnp.where(
                narrow == LANES - 1, pltpu.roll(y_recv[turn, 1, i], LANES - 1, 1), 0.0
            )
            if wide_y == LANES:
                halo_y = halo_low + halo_high
            else:
                middle = [jnp.zeros((wide_x, LANES), jnp.float32)] * (wide_y // LANES - 2)
                halo_y = jnp.concatenate([halo_low] + middle + [halo_high], 1)
            source = src[i] + spacing[i] * (coef_x * halo_x + coef_y * halo_y)
            src[i] = source
            first_value = first_value + low_w[i] * source
            last_value = last_value + high_w[i] * source

        slot = 1 + turn

        def up_value():
            ratio, gain, _ = up_factor()
            return gain * (up_recv[slot] + ratio * first_value) + last_value

        def down_value():
            ratio, gain, _ = down_factor()
            return gain * (down_recv[slot] + ratio * last_value) + first_value

        @pl.when((pz == 0) & (pz < nz - 1))
        def _():
            up_send[slot] = last_value
            up_copy(slot).start()

        @pl.when((pz == nz - 1) & (pz > 0))
        def _():
            down_send[slot] = first_value
            down_copy(slot).start()

        value = src[0] * inv[0]
        src[0] = value
        for i in range(1, depth):
            value = (src[i] + faces[i] * value) * inv[i]
            src[i] = value
        local[depth - 1] = value
        for i in range(depth - 2, -1, -1):
            value = src[i] + faces[i + 1] * inv[i] * value
            local[i] = value

        def pass_up():
            @pl.when(pz > 0)
            def _():
                if turn == 0:
                    up_copy(0).wait_recv()

                    @pl.when(pz < nz - 1)
                    def _():
                        up_send[0] = up_factor()[2]
                        up_copy(0).start()

                up_copy(slot).wait_recv()

                @pl.when(pz < nz - 1)
                def _():
                    up_send[slot] = up_value()
                    up_copy(slot).start()

        def pass_down():
            @pl.when(pz < nz - 1)
            def _():
                if turn == 0:
                    down_copy(0).wait_recv()

                    @pl.when(pz > 0)
                    def _():
                        down_send[0] = down_factor()[2]
                        down_copy(0).start()

                down_copy(slot).wait_recv()

                @pl.when(pz > 0)
                def _():
                    down_send[slot] = down_value()
                    down_copy(slot).start()

        upper_half = 2 * pz > nz - 1

        @pl.when(upper_half)
        def _():
            pass_down()

        pass_up()

        @pl.when(jnp.logical_not(upper_half))
        def _():
            pass_down()

        up_ratio, up_gain, up_next = up_factor()
        down_ratio = down_recv[0]
        below, above = up_recv[slot], down_recv[slot]
        carried = up_gain * (below + up_ratio * first_value) + last_value
        last_cell = (carried + up_next * above) / (1.0 - up_next * down_ratio)
        from_above = face_last * (down_ratio * last_cell + above)
        first_cell = (
            low_w[0] * face_first * below + first_both * from_above + first_value
        ) / (1.0 - low_w[0] * face_first * up_ratio)
        from_below = face_first * (up_ratio * first_cell + below)
        chosen = colour[...] == turn
        for i in range(depth):
            solved = local[i] + low_w[i] * from_below + high_w[i] * from_above
            fresh = jnp.where(chosen, solved, held[i])
            if turn == 0:
                iterate[i] = fresh
                x_send[1, 0, pl.ds(i, 1)] = fresh[0:1]
                x_send[1, 1, pl.ds(i, 1)] = fresh[wide_x - 1 : wide_x]
            else:
                out_ref[i] = fresh
        if turn == 0:
            send_halos(1)

    for turn in range(2):
        on_sides(px, nx, lambda side: x_copy(turn, side).wait_send())
        on_sides(py, ny, lambda side: y_copy(turn, side).wait_send())
    for slot in range(3):

        @pl.when(pz < nz - 1)
        def _():
            up_copy(slot).wait_send()

        @pl.when(pz > 0)
        def _():
            down_copy(slot).wait_send()


def on_device(counts, correction, residual, state, spacing_level, line_colour):
    block = correction.shape
    depth, wide_x, wide_y = block
    plane = (wide_x, wide_y)
    f32 = jnp.float32
    dma = pltpu.SemaphoreType.DMA
    anywhere = pl.BlockSpec(memory_space=pl.ANY)
    return pl.pallas_call(
        functools.partial(relax_kernel, counts),
        out_shape=jax.ShapeDtypeStruct(block, f32),
        in_specs=[pl.BlockSpec(memory_space=pltpu.SMEM)] + [anywhere] * 4,
        out_specs=pl.BlockSpec(memory_space=pltpu.VMEM),
        scratch_shapes=[
            pltpu.VMEM(block, f32),
            pltpu.VMEM(block, f32),
            pltpu.VMEM(block, f32),
            pltpu.VMEM(plane, jnp.int32),
            pltpu.VMEM(block, f32),
            pltpu.VMEM(block, f32),
            pltpu.VMEM(block, f32),
            pltpu.VMEM(block, f32),
            pltpu.VMEM(block, f32),
            pltpu.VMEM(block, f32),
            pltpu.VMEM((2, 2, depth, wide_y), f32),
            pltpu.VMEM((2, 2, depth, wide_y), f32),
            pltpu.VMEM((2, 2, depth, wide_x, LANES), f32),
            pltpu.VMEM((3,) + plane, f32),
            pltpu.VMEM((3,) + plane, f32),
            pltpu.VMEM((3,) + plane, f32),
            pltpu.VMEM((3,) + plane, f32),
            dma((4,)),
            dma((2, 2)),
            dma((2, 2)),
            dma((2, 2)),
            dma((2, 2)),
            dma((3,)),
            dma((3,)),
            dma((3,)),
            dma((3,)),
        ],
        compiler_params=pltpu.CompilerParams(collective_id=0, has_side_effects=True),
    )(spacing_level, correction, residual, state, line_colour)


def solution(mesh):
    counts = tuple(mesh.shape[a] for a in ("gx", "gy", "gz"))
    return jax.shard_map(
        functools.partial(on_device, counts),
        mesh=mesh,
        in_specs=(
            P("gz", "gx", "gy"),
            P("gz", "gx", "gy"),
            P("gz", "gx", "gy"),
            P(),
            P("gx", "gy"),
        ),
        out_specs=P("gz", "gx", "gy"),
        check_vma=False,
    )
```

```python
import functools

import jax
import jax.numpy as jnp
import numpy as np
from jax import lax
from jax.experimental import pallas as pl
from jax.experimental.pallas import tpu as pltpu
from jax.sharding import PartitionSpec as P

coef_z = 1000.0
coef_x = 0.3
coef_y = 0.2
bratu_lambda = 0.2
LANES = 128
MESH = pl.DeviceIdType.MESH


def relax_kernel(
    counts,
    level_ref,
    corr_hbm,
    res_hbm,
    state_hbm,
    colour_hbm,
    out_ref,
    corr,
    res,
    state,
    colour,
    iterate,
    inv,
    low_w,
    high_w,
    src,
    local,
    x_send,
    x_recv,
    y_recv,
    factor_send,
    factor_recv,
    gains,
    sum_send,
    sum_recv,
    load_sem,
    x_send_sem,
    x_recv_sem,
    y_send_sem,
    y_recv_sem,
    factor_send_sem,
    factor_recv_sem,
    sum_send_sem,
    sum_recv_sem,
):
    nx, ny, nz = counts
    depth, wide_x, wide_y = corr.shape
    px, py, pz = (lax.axis_index(a) for a in ("gx", "gy", "gz"))
    total = depth * nz

    axes = (("gx", px, nx), ("gy", py, ny))
    barrier = pltpu.get_barrier_semaphore()
    present = jnp.int32(0)
    for axis, place, count in axes:
        present = present + jnp.where(place > 0, 1, 0) + jnp.where(place < count - 1, 1, 0)

        @pl.when(place > 0)
        def _():
            pl.semaphore_signal(barrier, inc=1, device_id={axis: place - 1}, device_id_type=MESH)

        @pl.when(place < count - 1)
        def _():
            pl.semaphore_signal(barrier, inc=1, device_id={axis: place + 1}, device_id_type=MESH)

    for step in range(1, nz):
        present = present + jnp.where(pz >= step, 1, 0) + jnp.where(pz + step < nz, 1, 0)

        @pl.when(pz >= step)
        def _():
            pl.semaphore_signal(barrier, inc=1, device_id={"gz": pz - step}, device_id_type=MESH)

        @pl.when(pz + step < nz)
        def _():
            pl.semaphore_signal(barrier, inc=1, device_id={"gz": pz + step}, device_id_type=MESH)

    loads = [
        pltpu.make_async_copy(a, b, load_sem.at[n])
        for n, (a, b) in enumerate(
            ((state_hbm, state), (corr_hbm, corr), (res_hbm, res), (colour_hbm, colour))
        )
    ]
    for load in loads:
        load.start()

    for side, gone in ((0, px == 0), (1, px == nx - 1)):

        @pl.when(gone)
        def _():
            for turn in range(2):
                x_recv[turn, side] = jnp.zeros((depth, wide_y), jnp.float32)

    for side, gone in ((0, py == 0), (1, py == ny - 1)):

        @pl.when(gone)
        def _():
            for turn in range(2):
                y_recv[turn, side] = jnp.zeros((depth, wide_x, LANES), jnp.float32)

    ends = (pz == 0, pz == nz - 1)
    below_count = (pz, nz - 1 - pz)
    for way in range(2):

        @pl.when(ends[way])
        def _():
            factor_recv[way] = jnp.zeros(factor_recv.shape[1:], jnp.float32)

        for step in range(1, nz):

            @pl.when(below_count[way] < step)
            def _():
                for turn in range(2):
                    sum_recv[turn, way, step - 1] = jnp.zeros((wide_x, wide_y), jnp.float32)

    def spread(tile):
        row = jnp.concatenate([tile] * (wide_y // LANES), 1)
        return jnp.concatenate([row] * (wide_x // 8), 0)

    powers = [np.float32(0.8) * np.float32(1.3**n) for n in range(4)]

    def spacing_at(index):
        level = level_ref[index]
        value = jnp.where(level == 0, powers[0], powers[1])
        value = jnp.where(level == 2, powers[2], value)
        return jnp.where(level == 3, powers[3], value)

    base = pz * depth
    spacing = [spacing_at(base + i) for i in range(depth)]
    before = spacing_at(jnp.maximum(base - 1, 0))
    after = spacing_at(jnp.minimum(base + depth, total - 1))
    chain = [before] + spacing + [after]
    faces = []
    for i in range(depth + 1):
        face = coef_z * 2.0 / jnp.full((8, LANES), chain[i] + chain[i + 1], jnp.float32)
        if i == 0:
            face = jnp.where(pz == 0, 0.0, face)
        if i == depth:
            face = jnp.where(pz == nz - 1, 0.0, face)
        faces.append(spread(face))
    face_first, face_last = faces[0], faces[depth]

    loads[0].wait()
    for i in range(depth):
        state[i] = (faces[i] + faces[i + 1]) + spacing[i] * (
            2.0 * coef_x + 2.0 * coef_y - bratu_lambda * jnp.exp(state[i])
        )
    forward = 1.0 / state[0]
    backward = 1.0 / state[depth - 1]
    inv[0] = forward
    low_w[depth - 1] = backward
    for i in range(1, depth):
        forward = 1.0 / (state[i] - faces[i] * faces[i] * forward)
        inv[i] = forward
        j = depth - 1 - i
        backward = 1.0 / (state[j] - faces[j + 1] * faces[j + 1] * backward)
        low_w[j] = backward
    high_w[depth - 1] = forward
    for i in range(1, depth):
        backward = backward * faces[i] * low_w[i]
        low_w[i] = backward
        j = depth - 1 - i
        forward = forward * faces[j + 1] * inv[j]
        high_w[j] = forward

    def x_copy(turn, side):
        return pltpu.make_async_remote_copy(
            src_ref=x_send.at[turn, side],
            dst_ref=x_recv.at[turn, 1 - side],
            send_sem=x_send_sem.at[turn, side],
            recv_sem=x_recv_sem.at[turn, 1 - side],
            device_id={"gx": px - 1 if side == 0 else px + 1},
            device_id_type=MESH,
        )

    def y_copy(turn, side):
        whole = corr if turn == 0 else iterate
        start = 0 if side == 0 else wide_y - LANES
        return pltpu.make_async_remote_copy(
            src_ref=whole.at[:, :, pl.ds(start, LANES)],
            dst_ref=y_recv.at[turn, 1 - side],
            send_sem=y_send_sem.at[turn, side],
            recv_sem=y_recv_sem.at[turn, 1 - side],
            device_id={"gy": py - 1 if side == 0 else py + 1},
            device_id_type=MESH,
        )

    def factor_copy(way):
        return pltpu.make_async_remote_copy(
            src_ref=factor_send.at[way],
            dst_ref=factor_recv.at[way],
            send_sem=factor_send_sem.at[way],
            recv_sem=factor_recv_sem.at[way],
            device_id={"gz": pz + 1 - 2 * way},
            device_id_type=MESH,
        )

    def sum_copy(turn, way, step):
        return pltpu.make_async_remote_copy(
            src_ref=sum_send.at[turn, way],
            dst_ref=sum_recv.at[turn, way, step - 1],
            send_sem=sum_send_sem.at[turn, way, step - 1],
            recv_sem=sum_recv_sem.at[turn, way, step - 1],
            device_id={"gz": pz + step * (1 - 2 * way)},
            device_id_type=MESH,
        )

    def on_sides(place, count, action):
        for side, there in ((0, place > 0), (1, place < count - 1)):

            @pl.when(there)
            def _():
                action(side)

    def send_halos(turn):
        on_sides(px, nx, lambda side: x_copy(turn, side).start())
        on_sides(py, ny, lambda side: y_copy(turn, side).start())

    def wait_halos(turn):
        on_sides(py, ny, lambda side: y_copy(turn, 1 - side).wait_recv())
        on_sides(px, nx, lambda side: x_copy(turn, 1 - side).wait_recv())

    loads[1].wait()
    for i in range(depth):
        x_send[0, 0, pl.ds(i, 1)] = corr[i, pl.ds(0, 1)]
        x_send[0, 1, pl.ds(i, 1)] = corr[i, pl.ds(wide_x - 1, 1)]
    pl.semaphore_wait(barrier, present)
    send_halos(0)

    first_both = low_w[depth - 1]

    own = (low_w.at[0], high_w.at[depth - 1])
    near_face, far_face = (face_first, face_last), (face_last, face_first)

    def pass_factor(way):
        ratio, scale = factor_recv[way, 0], factor_recv[way, 1]
        gain = first_both * near_face[way] / (1.0 - own[way][...] * near_face[way] * ratio)
        ahead = far_face[way] * (own[1 - way][...] + first_both * gain * ratio)
        scale = jnp.where(ends[way], 1.0, gain * scale)
        gains[way, 0] = gain
        gains[way, 1] = gain * ratio
        gains[way, 2] = ahead
        gains[way, 3] = 1.0 / scale

        @pl.when(jnp.logical_not(ends[1 - way]))
        def _():
            factor_send[way, 0] = ahead
            factor_send[way, 1] = scale
            factor_copy(way).start()

    for way in range(2):

        @pl.when(ends[way])
        def _():
            pass_factor(way)

    loads[2].wait()
    loads[3].wait()

    rows = lax.broadcasted_iota(jnp.int32, (wide_x, wide_y), 0)
    columns = lax.broadcasted_iota(jnp.int32, (wide_x, wide_y), 1)
    narrow = lax.broadcasted_iota(jnp.int32, (wide_x, LANES), 1)
    x_first, x_last = rows == 0, rows == wide_x - 1
    y_first, y_last = columns == 0, columns == wide_y - 1

    for turn in range(2):
        held = corr if turn == 0 else iterate
        for i in range(depth):
            plane = held[i]
            beside = coef_x * (
                jnp.where(x_first, 0.0, pltpu.roll(plane, 1, 0))
                + jnp.where(x_last, 0.0, pltpu.roll(plane, wide_x - 1, 0))
            ) + coef_y * (
                jnp.where(y_first, 0.0, pltpu.roll(plane, 1, 1))
                + jnp.where(y_last, 0.0, pltpu.roll(plane, wide_y - 1, 1))
            )
            src[i] = spacing[i] * (res[i] + beside)
        wait_halos(turn)
        first_value = jnp.zeros((wide_x, wide_y), jnp.float32)
        last_value = first_value
        for i in range(depth):
            halo_x = jnp.where(
                x_first,
                x_recv[turn, 0, pl.ds(i, 1)],
                jnp.where(x_last, x_recv[turn, 1, pl.ds(i, 1)], 0.0),
            )
            halo_low = jnp.where(narrow == 0, pltpu.roll(y_recv[turn, 0, i], 1, 1), 0.0)
            halo_high = jnp.where(
                narrow == LANES - 1, pltpu.roll(y_recv[turn, 1, i], LANES - 1, 1), 0.0
            )
            if wide_y == LANES:
                halo_y = halo_low + halo_high
            else:
                middle = [jnp.zeros((wide_x, LANES), jnp.float32)] * (wide_y // LANES - 2)
                halo_y = jnp.concatenate([halo_low] + middle + [halo_high], 1)
            source = src[i] + spacing[i] * (coef_x * halo_x + coef_y * halo_y)
            src[i] = source
            first_value = first_value + low_w[i] * source
            last_value = last_value + high_w[i] * source

        edge_values = (first_value, last_value)

        def send_sums(way):
            @pl.when(jnp.logical_not(ends[1 - way]))
            def _():
                sum_send[turn, way] = gains[way, 3] * (
                    gains[way, 1] * edge_values[way] + edge_values[1 - way]
                )
                for step in range(nz - 1, 0, -1):

                    @pl.when(below_count[1 - way] >= step)
                    def _():
                        sum_copy(turn, way, step).start()

        def advance(way):
            @pl.when(jnp.logical_not(ends[way]))
            def _():
                factor_copy(way).wait_recv()
                pass_factor(way)

            send_sums(way)

        if turn == 0:
            upper_half = 2 * pz > nz - 1

            @pl.when(upper_half)
            def _():
                advance(1)

            advance(0)

            @pl.when(jnp.logical_not(upper_half))
            def _():
                advance(1)

        else:
            send_sums(0)
            send_sums(1)

        value = src[0] * inv[0]
        src[0] = value
        for i in range(1, depth):
            value = (src[i] + faces[i] * value) * inv[i]
            src[i] = value
        local[depth - 1] = value
        for i in range(depth - 2, -1, -1):
            value = src[i] + faces[i + 1] * inv[i] * value
            local[i] = value

        arrived = []
        for way in range(2):
            for step in range(1, nz):

                @pl.when(below_count[way] >= step)
                def _():
                    sum_copy(turn, way, step).wait_recv()

        for way in range(2):
            value = sum_recv[turn, way, 0]
            for step in range(2, nz):
                value = value + sum_recv[turn, way, step - 1]
            arrived.append(factor_recv[way, 1] * value)
        below, above = arrived
        up_ratio, down_ratio = factor_recv[0, 0], factor_recv[1, 0]
        up_next = gains[0, 2]
        carried = gains[0, 0] * below + gains[0, 1] * first_value + last_value
        last_cell = (carried + up_next * above) / (1.0 - up_next * down_ratio)
        from_above = face_last * (down_ratio * last_cell + above)
        first_cell = (
            low_w[0] * face_first * below + first_both * from_above + first_value
        ) / (1.0 - low_w[0] * face_first * up_ratio)
        from_below = face_first * (up_ratio * first_cell + below)
        chosen = colour[...] == turn
        for i in range(depth):
            solved = local[i] + low_w[i] * from_below + high_w[i] * from_above
            fresh = jnp.where(chosen, solved, held[i])
            if turn == 0:
                iterate[i] = fresh
                x_send[1, 0, pl.ds(i, 1)] = fresh[0:1]
                x_send[1, 1, pl.ds(i, 1)] = fresh[wide_x - 1 : wide_x]
            else:
                out_ref[i] = fresh
        if turn == 0:
            send_halos(1)

    for turn in range(2):
        on_sides(px, nx, lambda side: x_copy(turn, side).wait_send())
        on_sides(py, ny, lambda side: y_copy(turn, side).wait_send())
    for way in range(2):

        @pl.when(jnp.logical_not(ends[1 - way]))
        def _():
            factor_copy(way).wait_send()

        for step in range(1, nz):

            @pl.when(below_count[1 - way] >= step)
            def _():
                for turn in range(2):
                    sum_copy(turn, way, step).wait_send()


def on_device(counts, correction, residual, state, spacing_level, line_colour):
    block = correction.shape
    depth, wide_x, wide_y = block
    plane = (wide_x, wide_y)
    f32 = jnp.float32
    dma = pltpu.SemaphoreType.DMA
    others = max(counts[2] - 1, 1)
    anywhere = pl.BlockSpec(memory_space=pl.ANY)
    return pl.pallas_call(
        functools.partial(relax_kernel, counts),
        out_shape=jax.ShapeDtypeStruct(block, f32),
        in_specs=[pl.BlockSpec(memory_space=pltpu.SMEM)] + [anywhere] * 4,
        out_specs=pl.BlockSpec(memory_space=pltpu.VMEM),
        scratch_shapes=[
            pltpu.VMEM(block, f32),
            pltpu.VMEM(block, f32),
            pltpu.VMEM(block, f32),
            pltpu.VMEM(plane, jnp.int32),
            pltpu.VMEM(block, f32),
            pltpu.VMEM(block, f32),
            pltpu.VMEM(block, f32),
            pltpu.VMEM(block, f32),
            pltpu.VMEM(block, f32),
            pltpu.VMEM(block, f32),
            pltpu.VMEM((2, 2, depth, wide_y), f32),
            pltpu.VMEM((2, 2, depth, wide_y), f32),
            pltpu.VMEM((2, 2, depth, wide_x, LANES), f32),
            pltpu.VMEM((2, 2) + plane, f32),
            pltpu.VMEM((2, 2) + plane, f32),
            pltpu.VMEM((2, 4) + plane, f32),
            pltpu.VMEM((2, 2) + plane, f32),
            pltpu.VMEM((2, 2, others) + plane, f32),
            dma((4,)),
            dma((2, 2)),
            dma((2, 2)),
            dma((2, 2)),
            dma((2, 2)),
            dma((2,)),
            dma((2,)),
            dma((2, 2, others)),
            dma((2, 2, others)),
        ],
        compiler_params=pltpu.CompilerParams(collective_id=0, has_side_effects=True),
    )(spacing_level, correction, residual, state, line_colour)


def solution(mesh):
    counts = tuple(mesh.shape[a] for a in ("gx", "gy", "gz"))
    return jax.shard_map(
        functools.partial(on_device, counts),
        mesh=mesh,
        in_specs=(
            P("gz", "gx", "gy"),
            P("gz", "gx", "gy"),
            P("gz", "gx", "gy"),
            P(),
            P("gx", "gy"),
        ),
        out_specs=P("gz", "gx", "gy"),
        check_vma=False,
    )
```

```python
import functools

import jax
import jax.numpy as jnp
import numpy as np
from jax import lax
from jax.experimental import pallas as pl
from jax.experimental.pallas import tpu as pltpu
from jax.sharding import PartitionSpec as P

coef_z = 1000.0
coef_x = 0.3
coef_y = 0.2
bratu_lambda = 0.2
LANES = 128
MESH = pl.DeviceIdType.MESH


def relax_kernel(
    counts,
    level_ref,
    corr_hbm,
    res_hbm,
    state_hbm,
    colour_hbm,
    out_ref,
    corr,
    res,
    state,
    colour,
    iterate,
    low_w,
    grow,
    grow_scale,
    high_last,
    src,
    local,
    x_send,
    x_recv,
    y_recv,
    factor_send,
    factor_recv,
    gains,
    sum_send,
    sum_recv,
    load_sem,
    x_send_sem,
    x_recv_sem,
    y_send_sem,
    y_recv_sem,
    factor_send_sem,
    factor_recv_sem,
    sum_send_sem,
    sum_recv_sem,
):
    nx, ny, nz = counts
    depth, wide_x, wide_y = corr.shape
    px, py, pz = (lax.axis_index(a) for a in ("gx", "gy", "gz"))
    total = depth * nz

    axes = (("gx", px, nx), ("gy", py, ny))
    barrier = pltpu.get_barrier_semaphore()
    present = jnp.int32(0)
    for axis, place, count in axes:
        present = present + jnp.where(place > 0, 1, 0) + jnp.where(place < count - 1, 1, 0)

        @pl.when(place > 0)
        def _():
            pl.semaphore_signal(barrier, inc=1, device_id={axis: place - 1}, device_id_type=MESH)

        @pl.when(place < count - 1)
        def _():
            pl.semaphore_signal(barrier, inc=1, device_id={axis: place + 1}, device_id_type=MESH)

    for step in range(1, nz):
        present = present + jnp.where(pz >= step, 1, 0) + jnp.where(pz + step < nz, 1, 0)

        @pl.when(pz >= step)
        def _():
            pl.semaphore_signal(barrier, inc=1, device_id={"gz": pz - step}, device_id_type=MESH)

        @pl.when(pz + step < nz)
        def _():
            pl.semaphore_signal(barrier, inc=1, device_id={"gz": pz + step}, device_id_type=MESH)

    loads = [
        pltpu.make_async_copy(a, b, load_sem.at[n])
        for n, (a, b) in enumerate(
            ((state_hbm, state), (corr_hbm, corr), (res_hbm, res), (colour_hbm, colour))
        )
    ]
    for load in loads:
        load.start()

    for side, gone in ((0, px == 0), (1, px == nx - 1)):

        @pl.when(gone)
        def _():
            for turn in range(2):
                x_recv[turn, side] = jnp.zeros((depth, wide_y), jnp.float32)

    for side, gone in ((0, py == 0), (1, py == ny - 1)):

        @pl.when(gone)
        def _():
            for turn in range(2):
                y_recv[turn, side] = jnp.zeros((depth, wide_x, LANES), jnp.float32)

    ends = (pz == 0, pz == nz - 1)
    below_count = (pz, nz - 1 - pz)
    for way in range(2):

        @pl.when(ends[way])
        def _():
            factor_recv[way] = jnp.zeros(factor_recv.shape[1:], jnp.float32)

        for step in range(1, nz):

            @pl.when(below_count[way] < step)
            def _():
                for turn in range(2):
                    sum_recv[turn, way, step - 1] = jnp.zeros((wide_x, wide_y), jnp.float32)

    def spread(tile):
        row = jnp.concatenate([tile] * (wide_y // LANES), 1)
        return jnp.concatenate([row] * (wide_x // 8), 0)

    powers = [np.float32(0.8) * np.float32(1.3**n) for n in range(4)]

    def spacing_at(index):
        level = level_ref[index]
        value = jnp.where(level == 0, powers[0], powers[1])
        value = jnp.where(level == 2, powers[2], value)
        return jnp.where(level == 3, powers[3], value)

    base = pz * depth
    spacing = [spacing_at(base + i) for i in range(depth)]
    before = spacing_at(jnp.maximum(base - 1, 0))
    after = spacing_at(jnp.minimum(base + depth, total - 1))
    chain = [before] + spacing + [after]
    faces, widths = [], []
    for i in range(depth + 1):
        width = jnp.full((8, LANES), chain[i] + chain[i + 1], jnp.float32)
        face = coef_z * 2.0 / width
        if i == 0:
            face = jnp.where(pz == 0, 0.0, face)
        if i == depth:
            face = jnp.where(pz == nz - 1, 0.0, face)
        faces.append(spread(face))
        widths.append(spread(width * (0.5 / coef_z)))
    face_first, face_last = faces[0], faces[depth]

    loads[1].wait()
    for i in range(depth):
        x_send[0, 0, pl.ds(i, 1)] = corr[i, pl.ds(0, 1)]
        x_send[0, 1, pl.ds(i, 1)] = corr[i, pl.ds(wide_x - 1, 1)]
    loads[0].wait()
    for i in range(depth):
        state[i] = (faces[i] + faces[i + 1]) + spacing[i] * (
            2.0 * coef_x + 2.0 * coef_y - bratu_lambda * jnp.exp(state[i])
        )
    fore_last, fore = jnp.zeros((wide_x, wide_y), jnp.float32), None
    back_last, back = fore_last, None
    for i in range(depth):
        j = depth - 1 - i
        if i == 0:
            fore = back = jnp.ones((wide_x, wide_y), jnp.float32)
        else:
            fore_last, fore = fore, fore_next * widths[i]
            back_last, back = back, back_next * widths[j + 1]
        grow[i] = fore
        low_w[j] = back
        fore_next = state[i] * fore
        back_next = state[j] * back
        if i > 0:
            fore_next = fore_next - faces[i] * fore_last
            back_next = back_next - faces[j + 1] * back_last
    grow_scale[...] = 1.0 / fore_next
    back_scale = 1.0 / back_next
    for i in range(depth):
        low_w[i] = low_w[i] * back_scale
    high_last[...] = grow[depth - 1] * grow_scale[...]

    def x_copy(turn, side):
        return pltpu.make_async_remote_copy(
            src_ref=x_send.at[turn, side],
            dst_ref=x_recv.at[turn, 1 - side],
            send_sem=x_send_sem.at[turn, side],
            recv_sem=x_recv_sem.at[turn, 1 - side],
            device_id={"gx": px - 1 if side == 0 else px + 1},
            device_id_type=MESH,
        )

    def y_copy(turn, side):
        whole = corr if turn == 0 else iterate
        start = 0 if side == 0 else wide_y - LANES
        return pltpu.make_async_remote_copy(
            src_ref=whole.at[:, :, pl.ds(start, LANES)],
            dst_ref=y_recv.at[turn, 1 - side],
            send_sem=y_send_sem.at[turn, side],
            recv_sem=y_recv_sem.at[turn, 1 - side],
            device_id={"gy": py - 1 if side == 0 else py + 1},
            device_id_type=MESH,
        )

    def factor_copy(way, part):
        return pltpu.make_async_remote_copy(
            src_ref=factor_send.at[way, part],
            dst_ref=factor_recv.at[way, part],
            send_sem=factor_send_sem.at[way, part],
            recv_sem=factor_recv_sem.at[way, part],
            device_id={"gz": pz + 1 - 2 * way},
            device_id_type=MESH,
        )

    def sum_copy(turn, way, step):
        return pltpu.make_async_remote_copy(
            src_ref=sum_send.at[turn, way],
            dst_ref=sum_recv.at[turn, way, step - 1],
            send_sem=sum_send_sem.at[turn, way, step - 1],
            recv_sem=sum_recv_sem.at[turn, way, step - 1],
            device_id={"gz": pz + step * (1 - 2 * way)},
            device_id_type=MESH,
        )

    def on_sides(place, count, action):
        for side, there in ((0, place > 0), (1, place < count - 1)):

            @pl.when(there)
            def _():
                action(side)

    def send_halos(turn):
        on_sides(px, nx, lambda side: x_copy(turn, side).start())
        on_sides(py, ny, lambda side: y_copy(turn, side).start())

    def wait_halos(turn):
        on_sides(py, ny, lambda side: y_copy(turn, 1 - side).wait_recv())
        on_sides(px, nx, lambda side: x_copy(turn, 1 - side).wait_recv())

    pl.semaphore_wait(barrier, present)
    send_halos(0)

    first_both = low_w[depth - 1]

    own = (low_w.at[0], high_last)
    near_face, far_face = (face_first, face_last), (face_last, face_first)

    def pass_factor(way):
        ratio = factor_recv[way, 0]
        gain = first_both * near_face[way] / (1.0 - own[way][...] * near_face[way] * ratio)
        ahead = far_face[way] * (own[1 - way][...] + first_both * gain * ratio)

        @pl.when(jnp.logical_not(ends[1 - way]))
        def _():
            factor_send[way, 0] = ahead
            factor_copy(way, 0).start()

        gains[way, 0] = gain
        gains[way, 1] = gain * ratio
        gains[way, 2] = ahead

    def pass_scale(way):
        scale = jnp.where(ends[way], 1.0, gains[way, 0] * factor_recv[way, 1])

        @pl.when(jnp.logical_not(ends[1 - way]))
        def _():
            factor_send[way, 1] = scale
            factor_copy(way, 1).start()

        gains[way, 3] = 1.0 / scale

    for way in range(2):

        @pl.when(ends[way])
        def _():
            pass_factor(way)
            pass_scale(way)

    loads[2].wait()
    loads[3].wait()

    rows = lax.broadcasted_iota(jnp.int32, (wide_x, wide_y), 0)
    columns = lax.broadcasted_iota(jnp.int32, (wide_x, wide_y), 1)
    narrow = lax.broadcasted_iota(jnp.int32, (wide_x, LANES), 1)
    x_first, x_last = rows == 0, rows == wide_x - 1
    y_first, y_last = columns == 0, columns == wide_y - 1

    for turn in range(2):
        held = corr if turn == 0 else iterate
        for i in range(depth):
            plane = held[i]
            beside = coef_x * (
                jnp.where(x_first, 0.0, pltpu.roll(plane, 1, 0))
                + jnp.where(x_last, 0.0, pltpu.roll(plane, wide_x - 1, 0))
            ) + coef_y * (
                jnp.where(y_first, 0.0, pltpu.roll(plane, 1, 1))
                + jnp.where(y_last, 0.0, pltpu.roll(plane, wide_y - 1, 1))
            )
            src[i] = spacing[i] * (res[i] + beside)
        wait_halos(turn)
        first_value = jnp.zeros((wide_x, wide_y), jnp.float32)
        last_sum = first_value
        for i in range(depth):
            halo_x = jnp.where(
                x_first,
                x_recv[turn, 0, pl.ds(i, 1)],
                jnp.where(x_last, x_recv[turn, 1, pl.ds(i, 1)], 0.0),
            )
            halo_low = jnp.where(narrow == 0, pltpu.roll(y_recv[turn, 0, i], 1, 1), 0.0)
            halo_high = jnp.where(
                narrow == LANES - 1, pltpu.roll(y_recv[turn, 1, i], LANES - 1, 1), 0.0
            )
            if wide_y == LANES:
                halo_y = halo_low + halo_high
            else:
                middle = [jnp.zeros((wide_x, LANES), jnp.float32)] * (wide_y // LANES - 2)
                halo_y = jnp.concatenate([halo_low] + middle + [halo_high], 1)
            source = src[i] + spacing[i] * (coef_x * halo_x + coef_y * halo_y)
            src[i] = source
            first_value = first_value + low_w[i] * source
            local[i] = last_sum
            last_sum = last_sum + grow[i] * source

        last_value = last_sum * grow_scale[...]
        edge_values = (first_value, last_value)

        def send_sums(way):
            @pl.when(jnp.logical_not(ends[1 - way]))
            def _():
                sum_send[turn, way] = gains[way, 3] * (
                    gains[way, 1] * edge_values[way] + edge_values[1 - way]
                )
                for step in range(nz - 1, 0, -1):

                    @pl.when(below_count[1 - way] >= step)
                    def _():
                        sum_copy(turn, way, step).start()

        def advance(way):
            @pl.when(jnp.logical_not(ends[way]))
            def _():
                factor_copy(way, 0).wait_recv()
                pass_factor(way)
                factor_copy(way, 1).wait_recv()
                pass_scale(way)

            send_sums(way)

        if turn == 0:
            upper_half = 2 * pz > nz - 1

            @pl.when(upper_half)
            def _():
                advance(1)

            advance(0)

            @pl.when(jnp.logical_not(upper_half))
            def _():
                advance(1)

        else:
            send_sums(0)
            send_sums(1)

        arrived = []
        for way in range(2):
            for step in range(1, nz):

                @pl.when(below_count[way] >= step)
                def _():
                    sum_copy(turn, way, step).wait_recv()

        for way in range(2):
            value = sum_recv[turn, way, 0]
            for step in range(2, nz):
                value = value + sum_recv[turn, way, step - 1]
            arrived.append(factor_recv[way, 1] * value)
        below, above = arrived
        up_ratio, down_ratio = factor_recv[0, 0], factor_recv[1, 0]
        up_next = gains[0, 2]
        carried = gains[0, 0] * below + gains[0, 1] * first_value + last_value
        last_cell = (carried + up_next * above) / (1.0 - up_next * down_ratio)
        from_above = face_last * (down_ratio * last_cell + above)
        first_cell = (
            low_w[0] * face_first * below + first_both * from_above + first_value
        ) / (1.0 - low_w[0] * face_first * up_ratio)
        from_below = face_first * (up_ratio * first_cell + below)
        chosen = colour[...] == turn
        ahead_sum = from_above * grow_scale[...]
        for i in range(depth - 1, -1, -1):
            ahead_sum = ahead_sum + low_w[i] * src[i]
            solved = grow[i] * ahead_sum + low_w[i] * (local[i] + from_below)
            fresh = jnp.where(chosen, solved, held[i])
            if turn == 0:
                iterate[i] = fresh
                x_send[1, 0, pl.ds(i, 1)] = fresh[0:1]
                x_send[1, 1, pl.ds(i, 1)] = fresh[wide_x - 1 : wide_x]
            else:
                out_ref[i] = fresh
        if turn == 0:
            send_halos(1)

    for turn in range(2):
        on_sides(px, nx, lambda side: x_copy(turn, side).wait_send())
        on_sides(py, ny, lambda side: y_copy(turn, side).wait_send())
    for way in range(2):

        @pl.when(jnp.logical_not(ends[1 - way]))
        def _():
            factor_copy(way, 0).wait_send()
            factor_copy(way, 1).wait_send()

        for step in range(1, nz):

            @pl.when(below_count[1 - way] >= step)
            def _():
                for turn in range(2):
                    sum_copy(turn, way, step).wait_send()


def on_device(counts, correction, residual, state, spacing_level, line_colour):
    block = correction.shape
    depth, wide_x, wide_y = block
    plane = (wide_x, wide_y)
    f32 = jnp.float32
    dma = pltpu.SemaphoreType.DMA
    others = max(counts[2] - 1, 1)
    anywhere = pl.BlockSpec(memory_space=pl.ANY)
    return pl.pallas_call(
        functools.partial(relax_kernel, counts),
        out_shape=pltpu.VMEM(block, f32),
        in_specs=[pl.BlockSpec(memory_space=pltpu.SMEM)] + [anywhere] * 4,
        out_specs=pl.BlockSpec(memory_space=pltpu.VMEM),
        scratch_shapes=[
            pltpu.VMEM(block, f32),
            pltpu.VMEM(block, f32),
            pltpu.VMEM(block, f32),
            pltpu.VMEM(plane, jnp.int32),
            pltpu.VMEM(block, f32),
            pltpu.VMEM(block, f32),
            pltpu.VMEM(block, f32),
            pltpu.VMEM(plane, f32),
            pltpu.VMEM(plane, f32),
            pltpu.VMEM(block, f32),
            pltpu.VMEM(block, f32),
            pltpu.VMEM((2, 2, depth, wide_y), f32),
            pltpu.VMEM((2, 2, depth, wide_y), f32),
            pltpu.VMEM((2, 2, depth, wide_x, LANES), f32),
            pltpu.VMEM((2, 2) + plane, f32),
            pltpu.VMEM((2, 2) + plane, f32),
            pltpu.VMEM((2, 4) + plane, f32),
            pltpu.VMEM((2, 2) + plane, f32),
            pltpu.VMEM((2, 2, others) + plane, f32),
            dma((4,)),
            dma((2, 2)),
            dma((2, 2)),
            dma((2, 2)),
            dma((2, 2)),
            dma((2, 2)),
            dma((2, 2)),
            dma((2, 2, others)),
            dma((2, 2, others)),
        ],
        compiler_params=pltpu.CompilerParams(collective_id=0, has_side_effects=True),
    )(spacing_level, correction, residual, state, line_colour)


def solution(mesh):
    counts = tuple(mesh.shape[a] for a in ("gx", "gy", "gz"))
    return jax.shard_map(
        functools.partial(on_device, counts),
        mesh=mesh,
        in_specs=(
            P("gz", "gx", "gy"),
            P("gz", "gx", "gy"),
            P("gz", "gx", "gy"),
            P(),
            P("gx", "gy"),
        ),
        out_specs=P("gz", "gx", "gy"),
        check_vma=False,
    )
```

```python
import functools

import jax
import jax.numpy as jnp
import numpy as np
from jax import lax
from jax.experimental import pallas as pl
from jax.experimental.pallas import tpu as pltpu
from jax.sharding import PartitionSpec as P

coef_z = 1000.0
coef_x = 0.3
coef_y = 0.2
bratu_lambda = 0.2
LANES = 128
MESH = pl.DeviceIdType.MESH


def relax_kernel(
    counts,
    level_ref,
    corr_hbm,
    res_hbm,
    state_hbm,
    colour_hbm,
    out_ref,
    corr,
    res,
    state,
    colour,
    iterate,
    low_w,
    grow,
    grow_scale,
    high_last,
    src,
    local,
    x_send,
    x_recv,
    y_recv,
    factor_send,
    factor_recv,
    local_send,
    local_recv,
    behind,
    gains,
    sum_send,
    sum_recv,
    load_sem,
    x_send_sem,
    x_recv_sem,
    y_send_sem,
    y_recv_sem,
    factor_send_sem,
    factor_recv_sem,
    local_send_sem,
    local_recv_sem,
    sum_send_sem,
    sum_recv_sem,
):
    nx, ny, nz = counts
    depth, wide_x, wide_y = corr.shape
    px, py, pz = (lax.axis_index(a) for a in ("gx", "gy", "gz"))
    total = depth * nz

    axes = (("gx", px, nx), ("gy", py, ny))
    barrier = pltpu.get_barrier_semaphore()
    present = jnp.int32(0)
    for axis, place, count in axes:
        present = present + jnp.where(place > 0, 1, 0) + jnp.where(place < count - 1, 1, 0)

        @pl.when(place > 0)
        def _():
            pl.semaphore_signal(barrier, inc=1, device_id={axis: place - 1}, device_id_type=MESH)

        @pl.when(place < count - 1)
        def _():
            pl.semaphore_signal(barrier, inc=1, device_id={axis: place + 1}, device_id_type=MESH)

    for step in range(1, nz):
        present = present + jnp.where(pz >= step, 1, 0) + jnp.where(pz + step < nz, 1, 0)

        @pl.when(pz >= step)
        def _():
            pl.semaphore_signal(barrier, inc=1, device_id={"gz": pz - step}, device_id_type=MESH)

        @pl.when(pz + step < nz)
        def _():
            pl.semaphore_signal(barrier, inc=1, device_id={"gz": pz + step}, device_id_type=MESH)

    loads = [
        pltpu.make_async_copy(a, b, load_sem.at[n])
        for n, (a, b) in enumerate(
            ((state_hbm, state), (corr_hbm, corr), (res_hbm, res), (colour_hbm, colour))
        )
    ]
    for load in loads:
        load.start()

    for side, gone in ((0, px == 0), (1, px == nx - 1)):

        @pl.when(gone)
        def _():
            for turn in range(2):
                x_recv[turn, side] = jnp.zeros((depth, wide_y), jnp.float32)

    for side, gone in ((0, py == 0), (1, py == ny - 1)):

        @pl.when(gone)
        def _():
            for turn in range(2):
                y_recv[turn, side] = jnp.zeros((depth, wide_x, LANES), jnp.float32)

    ends = (pz == 0, pz == nz - 1)
    below_count = (pz, nz - 1 - pz)
    for way in range(2):

        for step in range(1, nz):

            @pl.when(below_count[way] < step)
            def _():
                for turn in range(2):
                    sum_recv[turn, way, step - 1] = jnp.zeros((wide_x, wide_y), jnp.float32)

    def spread(tile):
        row = jnp.concatenate([tile] * (wide_y // LANES), 1)
        return jnp.concatenate([row] * (wide_x // 8), 0)

    powers = [np.float32(0.8) * np.float32(1.3**n) for n in range(4)]

    def spacing_at(index):
        level = level_ref[index]
        value = jnp.where(level == 0, powers[0], powers[1])
        value = jnp.where(level == 2, powers[2], value)
        return jnp.where(level == 3, powers[3], value)

    base = pz * depth
    spacing = [spacing_at(base + i) for i in range(depth)]
    before = spacing_at(jnp.maximum(base - 1, 0))
    after = spacing_at(jnp.minimum(base + depth, total - 1))
    chain = [before] + spacing + [after]
    faces, widths = [], []
    for i in range(depth + 1):
        width = jnp.full((8, LANES), chain[i] + chain[i + 1], jnp.float32)
        face = coef_z * 2.0 / width
        if i == 0:
            face = jnp.where(pz == 0, 0.0, face)
        if i == depth:
            face = jnp.where(pz == nz - 1, 0.0, face)
        faces.append(spread(face))
        widths.append(spread(width * (0.5 / coef_z)))
    face_first, face_last = faces[0], faces[depth]

    loads[1].wait()
    for i in range(depth):
        x_send[0, 0, pl.ds(i, 1)] = corr[i, pl.ds(0, 1)]
        x_send[0, 1, pl.ds(i, 1)] = corr[i, pl.ds(wide_x - 1, 1)]
    loads[0].wait()
    for i in range(depth):
        state[i] = (faces[i] + faces[i + 1]) + spacing[i] * (
            2.0 * coef_x + 2.0 * coef_y - bratu_lambda * jnp.exp(state[i])
        )
    fore_last, fore = jnp.zeros((wide_x, wide_y), jnp.float32), None
    back_last, back = fore_last, None
    for i in range(depth):
        j = depth - 1 - i
        if i == 0:
            fore = back = jnp.ones((wide_x, wide_y), jnp.float32)
        else:
            fore_last, fore = fore, fore_next * widths[i]
            back_last, back = back, back_next * widths[j + 1]
        grow[i] = fore
        low_w[j] = back
        fore_next = state[i] * fore
        back_next = state[j] * back
        if i > 0:
            fore_next = fore_next - faces[i] * fore_last
            back_next = back_next - faces[j + 1] * back_last
    grow_scale[...] = 1.0 / fore_next
    back_scale = 1.0 / back_next
    for i in range(depth):
        low_w[i] = low_w[i] * back_scale
    high_last[...] = grow[depth - 1] * grow_scale[...]

    def x_copy(turn, side):
        return pltpu.make_async_remote_copy(
            src_ref=x_send.at[turn, side],
            dst_ref=x_recv.at[turn, 1 - side],
            send_sem=x_send_sem.at[turn, side],
            recv_sem=x_recv_sem.at[turn, 1 - side],
            device_id={"gx": px - 1 if side == 0 else px + 1},
            device_id_type=MESH,
        )

    def y_copy(turn, side):
        whole = corr if turn == 0 else iterate
        start = 0 if side == 0 else wide_y - LANES
        return pltpu.make_async_remote_copy(
            src_ref=whole.at[:, :, pl.ds(start, LANES)],
            dst_ref=y_recv.at[turn, 1 - side],
            send_sem=y_send_sem.at[turn, side],
            recv_sem=y_recv_sem.at[turn, 1 - side],
            device_id={"gy": py - 1 if side == 0 else py + 1},
            device_id_type=MESH,
        )

    def factor_copy(way, step):
        return pltpu.make_async_remote_copy(
            src_ref=factor_send.at[way],
            dst_ref=factor_recv.at[way],
            send_sem=factor_send_sem.at[way, step - 1],
            recv_sem=factor_recv_sem.at[way],
            device_id={"gz": pz + step * (1 - 2 * way)},
            device_id_type=MESH,
        )

    def local_copy(way):
        return pltpu.make_async_remote_copy(
            src_ref=local_send.at[way],
            dst_ref=local_recv.at[way],
            send_sem=local_send_sem.at[way],
            recv_sem=local_recv_sem.at[way],
            device_id={"gz": pz + 1 - 2 * way},
            device_id_type=MESH,
        )

    def sum_copy(turn, way, step):
        return pltpu.make_async_remote_copy(
            src_ref=sum_send.at[turn, way],
            dst_ref=sum_recv.at[turn, way, step - 1],
            send_sem=sum_send_sem.at[turn, way, step - 1],
            recv_sem=sum_recv_sem.at[turn, way, step - 1],
            device_id={"gz": pz + step * (1 - 2 * way)},
            device_id_type=MESH,
        )

    def on_sides(place, count, action):
        for side, there in ((0, place > 0), (1, place < count - 1)):

            @pl.when(there)
            def _():
                action(side)

    def send_halos(turn):
        on_sides(px, nx, lambda side: x_copy(turn, side).start())
        on_sides(py, ny, lambda side: y_copy(turn, side).start())

    def wait_halos(turn):
        on_sides(py, ny, lambda side: y_copy(turn, 1 - side).wait_recv())
        on_sides(px, nx, lambda side: x_copy(turn, 1 - side).wait_recv())

    pl.semaphore_wait(barrier, present)
    send_halos(0)

    first_both = low_w[depth - 1]

    own = (low_w.at[0], high_last)
    near_face, far_face = (face_first, face_last), (face_last, face_first)

    ahead_count = (below_count[1], below_count[0])
    odd = [lax.rem(below_count[way], 2) == 1 for way in range(2)]
    skipped = []
    for row in (base - depth, base + 2 * depth):
        low = jnp.clip(row - 1, 0, total - 1)
        high = jnp.clip(row, 0, total - 1)
        width = jnp.full((8, LANES), spacing_at(low) + spacing_at(high), jnp.float32)
        skipped.append(spread(coef_z * 2.0 / width))

    def pass_factor(way):
        ratio = behind[way, 0]
        gain = first_both * near_face[way] / (1.0 - own[way][...] * near_face[way] * ratio)
        ahead = far_face[way] * (own[1 - way][...] + first_both * gain * ratio)
        scale = jnp.where(ends[way], 1.0, gain * behind[way, 1])

        @pl.when(jnp.logical_not(odd[way]) & (ahead_count[way] >= 1))
        def _():
            factor_send[way, 0] = ahead
            factor_send[way, 1] = scale

            @pl.when(ahead_count[way] >= 2)
            def _():
                factor_copy(way, 2).start()

            factor_copy(way, 1).start()

        gains[way, 0] = gain
        gains[way, 1] = gain * ratio
        gains[way, 2] = ahead
        gains[way, 3] = 1.0 / scale

    def take_factor(way):
        @pl.when(odd[way])
        def _():
            factor_copy(way, 1).wait_recv()
            behind[way] = factor_recv[way]

        @pl.when(jnp.logical_not(odd[way]))
        def _():
            factor_copy(way, 2).wait_recv()
            local_copy(way).wait_recv()
            ratio = factor_recv[way, 0]
            both = local_recv[way, 1]
            gain = both * skipped[way] / (1.0 - local_recv[way, 0] * skipped[way] * ratio)
            behind[way, 0] = near_face[way] * (local_recv[way, 2] + both * gain * ratio)
            behind[way, 1] = gain * factor_recv[way, 1]

    for way in range(2):

        @pl.when(ends[way])
        def _():
            behind[way] = jnp.zeros(behind.shape[1:], jnp.float32)
            pass_factor(way)

        @pl.when(odd[way] & (ahead_count[way] >= 1))
        def _():
            local_send[way, 0] = own[way][...]
            local_send[way, 1] = first_both
            local_send[way, 2] = own[1 - way][...]
            local_copy(way).start()

    loads[2].wait()
    loads[3].wait()

    rows = lax.broadcasted_iota(jnp.int32, (wide_x, wide_y), 0)
    columns = lax.broadcasted_iota(jnp.int32, (wide_x, wide_y), 1)
    narrow = lax.broadcasted_iota(jnp.int32, (wide_x, LANES), 1)
    x_first, x_last = rows == 0, rows == wide_x - 1
    y_first, y_last = columns == 0, columns == wide_y - 1

    for turn in range(2):
        held = corr if turn == 0 else iterate
        for i in range(depth):
            plane = held[i]
            beside = coef_x * (
                jnp.where(x_first, 0.0, pltpu.roll(plane, 1, 0))
                + jnp.where(x_last, 0.0, pltpu.roll(plane, wide_x - 1, 0))
            ) + coef_y * (
                jnp.where(y_first, 0.0, pltpu.roll(plane, 1, 1))
                + jnp.where(y_last, 0.0, pltpu.roll(plane, wide_y - 1, 1))
            )
            src[i] = spacing[i] * (res[i] + beside)
        wait_halos(turn)
        first_value = jnp.zeros((wide_x, wide_y), jnp.float32)
        last_sum = first_value
        for i in range(depth):
            halo_x = jnp.where(
                x_first,
                x_recv[turn, 0, pl.ds(i, 1)],
                jnp.where(x_last, x_recv[turn, 1, pl.ds(i, 1)], 0.0),
            )
            halo_low = jnp.where(narrow == 0, pltpu.roll(y_recv[turn, 0, i], 1, 1), 0.0)
            halo_high = jnp.where(
                narrow == LANES - 1, pltpu.roll(y_recv[turn, 1, i], LANES - 1, 1), 0.0
            )
            if wide_y == LANES:
                halo_y = halo_low + halo_high
            else:
                middle = [jnp.zeros((wide_x, LANES), jnp.float32)] * (wide_y // LANES - 2)
                halo_y = jnp.concatenate([halo_low] + middle + [halo_high], 1)
            source = src[i] + spacing[i] * (coef_x * halo_x + coef_y * halo_y)
            src[i] = source
            first_value = first_value + low_w[i] * source
            local[i] = last_sum
            last_sum = last_sum + grow[i] * source

        last_value = last_sum * grow_scale[...]
        edge_values = (first_value, last_value)

        def send_sums(way):
            @pl.when(jnp.logical_not(ends[1 - way]))
            def _():
                sum_send[turn, way] = gains[way, 3] * (
                    gains[way, 1] * edge_values[way] + edge_values[1 - way]
                )
                for step in range(nz - 1, 0, -1):

                    @pl.when(below_count[1 - way] >= step)
                    def _():
                        sum_copy(turn, way, step).start()

        def advance(way):
            @pl.when(jnp.logical_not(ends[way]))
            def _():
                take_factor(way)
                pass_factor(way)

            send_sums(way)

        if turn == 0:
            upper_half = 2 * pz > nz - 1

            @pl.when(upper_half)
            def _():
                advance(1)

            advance(0)

            @pl.when(jnp.logical_not(upper_half))
            def _():
                advance(1)

        else:
            send_sums(0)
            send_sums(1)

        arrived = []
        for way in range(2):
            for step in range(1, nz):

                @pl.when(below_count[way] >= step)
                def _():
                    sum_copy(turn, way, step).wait_recv()

        for way in range(2):
            value = sum_recv[turn, way, 0]
            for step in range(2, nz):
                value = value + sum_recv[turn, way, step - 1]
            arrived.append(behind[way, 1] * value)
        below, above = arrived
        up_ratio, down_ratio = behind[0, 0], behind[1, 0]
        up_next = gains[0, 2]
        carried = gains[0, 0] * below + gains[0, 1] * first_value + last_value
        last_cell = (carried + up_next * above) / (1.0 - up_next * down_ratio)
        from_above = face_last * (down_ratio * last_cell + above)
        first_cell = (
            low_w[0] * face_first * below + first_both * from_above + first_value
        ) / (1.0 - low_w[0] * face_first * up_ratio)
        from_below = face_first * (up_ratio * first_cell + below)
        chosen = colour[...] == turn
        ahead_sum = from_above * grow_scale[...]
        for i in range(depth - 1, -1, -1):
            ahead_sum = ahead_sum + low_w[i] * src[i]
            solved = grow[i] * ahead_sum + low_w[i] * (local[i] + from_below)
            fresh = jnp.where(chosen, solved, held[i])
            if turn == 0:
                iterate[i] = fresh
                x_send[1, 0, pl.ds(i, 1)] = fresh[0:1]
                x_send[1, 1, pl.ds(i, 1)] = fresh[wide_x - 1 : wide_x]
            else:
                out_ref[i] = fresh
        if turn == 0:
            send_halos(1)

    for turn in range(2):
        on_sides(px, nx, lambda side: x_copy(turn, side).wait_send())
        on_sides(py, ny, lambda side: y_copy(turn, side).wait_send())
    for way in range(2):

        @pl.when(odd[way] & (ahead_count[way] >= 1))
        def _():
            local_copy(way).wait_send()

        for step in (1, 2):

            @pl.when(jnp.logical_not(odd[way]) & (ahead_count[way] >= step))
            def _():
                factor_copy(way, step).wait_send()

        for step in range(1, nz):

            @pl.when(below_count[1 - way] >= step)
            def _():
                for turn in range(2):
                    sum_copy(turn, way, step).wait_send()


def on_device(counts, correction, residual, state, spacing_level, line_colour):
    block = correction.shape
    depth, wide_x, wide_y = block
    plane = (wide_x, wide_y)
    f32 = jnp.float32
    dma = pltpu.SemaphoreType.DMA
    others = max(counts[2] - 1, 1)
    anywhere = pl.BlockSpec(memory_space=pl.ANY)
    return pl.pallas_call(
        functools.partial(relax_kernel, counts),
        out_shape=pltpu.VMEM(block, f32),
        in_specs=[pl.BlockSpec(memory_space=pltpu.SMEM)] + [anywhere] * 4,
        out_specs=pl.BlockSpec(memory_space=pltpu.VMEM),
        scratch_shapes=[
            pltpu.VMEM(block, f32),
            pltpu.VMEM(block, f32),
            pltpu.VMEM(block, f32),
            pltpu.VMEM(plane, jnp.int32),
            pltpu.VMEM(block, f32),
            pltpu.VMEM(block, f32),
            pltpu.VMEM(block, f32),
            pltpu.VMEM(plane, f32),
            pltpu.VMEM(plane, f32),
            pltpu.VMEM(block, f32),
            pltpu.VMEM(block, f32),
            pltpu.VMEM((2, 2, depth, wide_y), f32),
            pltpu.VMEM((2, 2, depth, wide_y), f32),
            pltpu.VMEM((2, 2, depth, wide_x, LANES), f32),
            pltpu.VMEM((2, 2) + plane, f32),
            pltpu.VMEM((2, 2) + plane, f32),
            pltpu.VMEM((2, 3) + plane, f32),
            pltpu.VMEM((2, 3) + plane, f32),
            pltpu.VMEM((2, 2) + plane, f32),
            pltpu.VMEM((2, 4) + plane, f32),
            pltpu.VMEM((2, 2) + plane, f32),
            pltpu.VMEM((2, 2, others) + plane, f32),
            dma((4,)),
            dma((2, 2)),
            dma((2, 2)),
            dma((2, 2)),
            dma((2, 2)),
            dma((2, 2)),
            dma((2,)),
            dma((2,)),
            dma((2,)),
            dma((2, 2, others)),
            dma((2, 2, others)),
        ],
        compiler_params=pltpu.CompilerParams(collective_id=0, has_side_effects=True),
    )(spacing_level, correction, residual, state, line_colour)


def solution(mesh):
    counts = tuple(mesh.shape[a] for a in ("gx", "gy", "gz"))
    return jax.shard_map(
        functools.partial(on_device, counts),
        mesh=mesh,
        in_specs=(
            P("gz", "gx", "gy"),
            P("gz", "gx", "gy"),
            P("gz", "gx", "gy"),
            P(),
            P("gx", "gy"),
        ),
        out_specs=P("gz", "gx", "gy"),
        check_vma=False,
    )
```
